32 devices in a mesh: rep: 4 (over z), px: 4 (over x, core), py: 2 (over y).
Axes of the slice: x: 2, y: 2, z: 4, core: 2. Of those that a mesh axis runs over, the one named last changes fastest.
Arguments:
- state: float32 [12, 2, 192, 96, 256], P('rep', None, 'px', 'py'), parts along dimension 0, may hold values from -6 to 6
- cotangent: float32 [12, 2, 192, 96, 256], P('rep', None, 'px', 'py'), parts along dimension 0, may hold values from -6 to 6
- w_in: bfloat16 [512, 192], replicated, may hold values from -0.4375 to 0.4375
- b_in: float32 [512], replicated, may hold values from -5 to 5
- w_out: bfloat16 [192, 512], replicated, may hold values from -0.25 to 0.25
Outputs:
- state_grad: float32 [12, 2, 192, 96, 256], P('rep', None, 'px', 'py'), parts along dimension 0
- grad_in: float32 [512, 768], P(('px', 'py'), 'rep'), parts along dimension 1
- grad_out: float32 [768, 512], P('rep', ('px', 'py')), parts along dimension 0
- grad_bias: float32 [4, 512], P('rep', ('px', 'py')), parts along dimension 0
The draws below stay inside these ranges and needn't reach their ends.
There are 4 independent parts, one for each index of `rep`. The reference program is written for one: setup_inputs(seed, part) draws one part's arguments, and reference() takes and returns one part's arrays. A program takes and returns all parts, laid end to end along the dimension named above; an argument that names none is the same for every part. Nothing has to cross between parts.
All inputs are finite; a program needn't handle non-finite values.
Results may differ from the reference program's by a relative error of at most 0.0065.
The reference program's roundings to bfloat16 on the way count: a program that leaves them out, or rounds other values in their place, can miss the bound.
Values may be sent and summed in bfloat16 or wider, within the bound.
A program may use at most 448 MiB of HBM per device.

```python
import math
import jax
import jax.numpy as jnp
from jax import lax

NG = 256
KY = 192
KZ = 96
PATCH = 4
FEAT = 192
HID = 512


def steps_of(rng, shape, cuts, smallest, largest):
    def one(position, blocks):
        heights = jax.random.uniform(jax.random.fold_in(jax.random.fold_in(rng, 6), position), (blocks,), jnp.float32, smallest / len(cuts), largest / len(cuts))
        return jnp.repeat(jnp.exp(heights), shape[position] // blocks).reshape((-1,) + (1,) * (len(shape) - position - 1))

    level = one(*cuts[0])
    for cut in cuts[1:]:
        level = level * one(*cut)
    return level


def centred(rng, dims, deviation, reach, pieces=(), held_as=jnp.bfloat16):
    drawn = jax.random.normal(rng, dims, jnp.float32) * deviation
    if len(pieces) > 0:
        drawn = steps_of(rng, dims, pieces, -0.22, 0.18) * drawn
    return jnp.clip(drawn, min=-reach, max=reach).astype(held_as)


def setup_inputs(seed: int = 0, part: int = 0) -> dict:
    seeds = jax.random.split(jax.random.key(seed), 6)
    own_keys = jax.random.split(jax.random.fold_in(seeds[5], part), 6)
    state = centred(own_keys[0], (3, 2, KY, KZ, NG), 1.3, 6.0, ((2, 4), (3, 2)), jnp.float32)
    cotangent = centred(own_keys[1], (3, 2, KY, KZ, NG), 1.0, 6.0, ((2, 4), (3, 2)), jnp.float32)
    w_in = centred(seeds[2], (HID, FEAT), FEAT ** -0.5, 0.4375)
    b_in = centred(seeds[3], (HID,), 1.0, 5.0, (), jnp.float32)
    w_out = centred(seeds[4], (FEAT, HID), HID ** -0.5, 0.25)
    return dict(state=state, cotangent=cotangent, w_in=w_in, b_in=b_in, w_out=w_out)


NU_DT = 5e-05
TIME_STEP = 0.01
FORCING = 20.0

def angles(leading, trailing, length):
    product = leading[:, None] * trailing[None, :] % length
    phases = product.astype(jnp.float32) * (2.0 * math.pi / length)
    factor = 1.0 / math.sqrt(length)
    return (jnp.cos(phases) * factor, jnp.sin(phases) * factor)

def mode_ids(count, length):
    counter = jnp.arange(count, dtype=jnp.int32)
    return jnp.where(counter < count // 2, counter, counter + length - count).astype(jnp.int32)

def mode_table(modes, length, direction):
    cosine, sine_part = angles(modes, jnp.arange(length, dtype=jnp.int32), length)
    top_rows = jnp.stack([cosine, direction * sine_part], axis=1)
    low_rows = jnp.stack([-direction * sine_part, cosine], axis=1)
    return jnp.stack([top_rows, low_rows], axis=0).astype(jnp.bfloat16)

def complex_table(length, direction):
    return mode_table(jnp.arange(length, dtype=jnp.int32), length, direction)

def real_table(length, mode_count):
    cosine, sine_part = angles(jnp.arange(mode_count, dtype=jnp.int32), jnp.arange(length, dtype=jnp.int32), length)
    return jnp.stack([cosine, -sine_part], axis=0).astype(jnp.bfloat16)

def rounded(values):
    return lax.optimization_barrier(values.astype(jnp.bfloat16)).astype(jnp.float32)

def signed(counter, length):
    return jnp.where(counter < length // 2, counter, counter - length).astype(jnp.float32)

def factors(ky_ids, kz_ids, length, ky_count):
    cutoff = length // 3
    wave_y = signed(ky_ids, ky_count)[:, None, None]
    wave_z = kz_ids.astype(jnp.float32)[None, :, None]
    wave_x = signed(jnp.arange(length, dtype=jnp.int32), length)[None, None, :]
    retained = ((jnp.abs(wave_x) <= cutoff) & (jnp.abs(wave_y) <= cutoff) & (wave_z <= cutoff)).astype(jnp.float32)
    square = wave_x * wave_x + wave_y * wave_y + wave_z * wave_z
    damping = jnp.exp(-NU_DT * square)
    weight = jnp.where(kz_ids[None, :, None] == 0, 1.0, 2.0).astype(jnp.float32)
    return ((wave_x, wave_y, wave_z), retained, damping, weight, square)

def cross(former, latter):
    return [former[1] * latter[2] - former[2] * latter[1], former[2] * latter[0] - former[0] * latter[2], former[0] * latter[1] - former[1] * latter[0]]

def curl_modes(waves, spectra):
    real_part = cross(waves, [spectra[slot, 0] for slot in range(3)])
    imag_part = cross(waves, [spectra[slot, 1] for slot in range(3)])
    return jnp.stack([jnp.stack([-imag_part[slot], real_part[slot]]) for slot in range(3)])

def project(waves, square, spectra):
    dotted = waves[0] * spectra[0] + waves[1] * spectra[1] + waves[2] * spectra[2]
    along_k = dotted / jnp.maximum(square, 1.0)
    return jnp.stack([spectra[slot] - waves[slot] * along_k for slot in range(3)])

def to_physical(spectra):
    length = spectra.shape[4]
    inverse = complex_table(length, 1.0).astype(jnp.float32)
    y_inverse = mode_table(mode_ids(spectra.shape[2], length), length, 1.0).astype(jnp.float32)
    z_table = real_table(length, spectra.shape[3]).astype(jnp.float32)
    sectioned = rounded(spectra)
    sectioned = rounded(jnp.einsum('cramn,rnsx->csamx', sectioned, inverse, precision=lax.Precision.HIGHEST))
    sectioned = rounded(jnp.einsum('csamx,saty->ctmxy', sectioned, y_inverse, precision=lax.Precision.HIGHEST))
    return jnp.einsum('ctmxy,tmz->cxyz', sectioned, z_table, precision=lax.Precision.HIGHEST).astype(jnp.bfloat16)

def to_spectral(field):
    length = field.shape[3]
    forward = complex_table(length, -1.0).astype(jnp.float32)
    y_forward = mode_table(mode_ids(KY, length), length, -1.0).astype(jnp.float32).transpose(0, 3, 2, 1)
    z_table = real_table(length, KZ).astype(jnp.float32)
    sectioned = field.astype(jnp.float32)
    sectioned = rounded(jnp.einsum('cxyz,rmz->crmxy', sectioned, z_table, precision=lax.Precision.HIGHEST))
    sectioned = rounded(jnp.einsum('crmxy,rysa->csamx', sectioned, y_forward, precision=lax.Precision.HIGHEST))
    return jnp.einsum('csamx,sxtn->ctamn', sectioned, forward, precision=lax.Precision.HIGHEST)

def to_boxes(field):
    channels, span_x, span_y, span_z = field.shape
    tiles = field.reshape(channels, span_x // PATCH, PATCH, span_y // PATCH, PATCH, span_z // PATCH, PATCH)
    return tiles.transpose(0, 2, 4, 6, 1, 3, 5).reshape(channels * PATCH ** 3, -1)

def from_boxes(box_values, layout):
    channels, span_x, span_y, span_z = layout
    tiles = box_values.reshape(channels, PATCH, PATCH, PATCH, span_x // PATCH, span_y // PATCH, span_z // PATCH)
    return tiles.transpose(0, 4, 1, 5, 2, 6, 3).reshape(layout)

def closure_terms(velocity, force_adj, w_in, b_in, w_out):
    features = to_boxes(velocity)
    adjoints = to_boxes(force_adj)
    pre_act = jnp.dot(w_in, features, preferred_element_type=jnp.float32) + b_in[:, None]
    hidden = jax.nn.silu(pre_act).astype(jnp.bfloat16)
    sigmoid = jax.nn.sigmoid(pre_act)
    hidden_adj = FORCING * jnp.dot(w_out.T, adjoints, preferred_element_type=jnp.float32)
    pre_adj = (hidden_adj * sigmoid * (1.0 + pre_act * (1.0 - sigmoid))).astype(jnp.bfloat16)
    grad_in = jnp.dot(pre_adj, features.T, preferred_element_type=jnp.float32)
    grad_out = FORCING * jnp.dot(adjoints, hidden.T, preferred_element_type=jnp.float32)
    grad_bias = lax.optimization_barrier(jnp.sum(pre_adj.astype(jnp.float32), axis=1))[None, :]
    feat_adj = jnp.dot(w_in.T, pre_adj, preferred_element_type=jnp.float32)
    return (from_boxes(feat_adj, velocity.shape), grad_in, grad_out, grad_bias)

def pointwise(feat_adj, velocity, vorticity, force_adj):
    vel_list = [velocity[slot].astype(jnp.float32) for slot in range(3)]
    vort_list = [vorticity[slot].astype(jnp.float32) for slot in range(3)]
    force_list = [force_adj[slot].astype(jnp.float32) for slot in range(3)]
    turned = cross(vort_list, force_list)
    vel_adj = jnp.stack([feat_adj[slot] + turned[slot] for slot in range(3)]).astype(jnp.bfloat16)
    vort_adj = jnp.stack(cross(force_list, vel_list)).astype(jnp.bfloat16)
    return (vel_adj, vort_adj)

def reference(state, cotangent, w_in, b_in, w_out):
    waves, retained, damping, weight, square = factors(jnp.arange(KY, dtype=jnp.int32), jnp.arange(KZ, dtype=jnp.int32), NG, KY)
    kept = retained * state
    spectra = weight * jnp.concatenate([kept, curl_modes(waves, kept)], axis=0)
    fields = to_physical(spectra)
    velocity, vorticity = (fields[:3], fields[3:])
    force_spec = TIME_STEP * retained * project(waves, square, damping * cotangent)
    force_adj = to_physical(force_spec)
    feat_adj, grad_in, grad_out, grad_bias = closure_terms(velocity, force_adj, w_in, b_in, w_out)
    vel_adj, vort_adj = pointwise(feat_adj, velocity, vorticity, force_adj)
    spectral = to_spectral(jnp.concatenate([vel_adj, vort_adj], axis=0))
    state_grad = damping * cotangent + weight * retained * (spectral[:3] + curl_modes(waves, spectral[3:]))
    return (state_grad, grad_in, grad_out, grad_bias)
```

```python
import math

import jax
import jax.numpy as jnp
from jax import lax
from jax.sharding import PartitionSpec as P

PATCH = 4


NU_DT = 5e-05
TIME_STEP = 0.01
FORCING = 20.0


def angles(leading, trailing, length):
    product = leading[:, None] * trailing[None, :] % length
    phases = product.astype(jnp.float32) * (2.0 * math.pi / length)
    factor = 1.0 / math.sqrt(length)
    return (jnp.cos(phases) * factor, jnp.sin(phases) * factor)


def mode_ids(count, length):
    counter = jnp.arange(count, dtype=jnp.int32)
    return jnp.where(counter < count // 2, counter, counter + length - count)


def mode_table(modes, length, direction):
    cosine, sine_part = angles(modes, jnp.arange(length, dtype=jnp.int32), length)
    top_rows = jnp.stack([cosine, direction * sine_part], axis=1)
    low_rows = jnp.stack([-direction * sine_part, cosine], axis=1)
    return jnp.stack([top_rows, low_rows], axis=0).astype(jnp.bfloat16)


def complex_table(length, direction):
    return mode_table(jnp.arange(length, dtype=jnp.int32), length, direction)


def real_table(length, mode_count):
    cosine, sine_part = angles(
        jnp.arange(mode_count, dtype=jnp.int32), jnp.arange(length, dtype=jnp.int32), length
    )
    return jnp.stack([cosine, -sine_part], axis=0).astype(jnp.bfloat16)


def box_order(length, span):
    counter = jnp.arange(length, dtype=jnp.int32)
    local = counter % span
    rows = span // PATCH
    return counter - local + local % rows * PATCH + local // rows


def signed(counter, length):
    return jnp.where(counter < length // 2, counter, counter - length).astype(jnp.float32)


def factors(ky_ids, kz_ids, length, ky_count):
    cutoff = length // 3
    wave_y = signed(ky_ids, ky_count)[:, None, None]
    wave_z = kz_ids.astype(jnp.float32)[None, :, None]
    wave_x = signed(jnp.arange(length, dtype=jnp.int32), length)[None, None, :]
    retained = (
        (jnp.abs(wave_x) <= cutoff) & (jnp.abs(wave_y) <= cutoff) & (wave_z <= cutoff)
    ).astype(jnp.float32)
    square = wave_x * wave_x + wave_y * wave_y + wave_z * wave_z
    damping = jnp.exp(-NU_DT * square)
    weight = jnp.where(kz_ids[None, :, None] == 0, 1.0, 2.0).astype(jnp.float32)
    return ((wave_x, wave_y, wave_z), retained, damping, weight, square)


def cross(former, latter):
    return [
        former[1] * latter[2] - former[2] * latter[1],
        former[2] * latter[0] - former[0] * latter[2],
        former[0] * latter[1] - former[1] * latter[0],
    ]


def curl_modes(waves, spectra):
    real_part = cross(waves, [spectra[slot, 0] for slot in range(3)])
    imag_part = cross(waves, [spectra[slot, 1] for slot in range(3)])
    return jnp.stack([jnp.stack([-imag_part[slot], real_part[slot]]) for slot in range(3)])


def project(waves, square, spectra):
    dotted = waves[0] * spectra[0] + waves[1] * spectra[1] + waves[2] * spectra[2]
    along_k = dotted / jnp.maximum(square, 1.0)
    return jnp.stack([spectra[slot] - waves[slot] * along_k for slot in range(3)])


def to_physical(spectra):
    channels, paired, width_y, width_z, length = spectra.shape
    parts_x = lax.axis_size("px")
    parts_y = lax.axis_size("py")
    order_y = box_order(length, length)
    order_z = box_order(length, length)
    inverse = complex_table(length, 1.0)
    y_table = mode_table(mode_ids(width_y * parts_x, length), length, 1.0)[..., order_y].reshape(
        2, parts_x, width_y, 2, length
    )
    z_table = real_table(length, width_z * parts_y)[..., order_z].reshape(
        2, parts_y, width_z, length
    )
    flat = spectra.astype(jnp.bfloat16).reshape(channels, paired, width_y * width_z, length)
    along_x = jnp.einsum(
        "crpn,rnsx->csxp", flat, inverse, preferred_element_type=jnp.float32
    ).astype(jnp.bfloat16)
    along_x = along_x.reshape(channels, 2, length, 1, width_y * width_z)
    moved = lax.all_to_all(along_x, ("px", "py"), split_axis=2, concat_axis=3, tiled=True)
    blocks = moved.reshape(moved.shape[0], 2, moved.shape[2], parts_x, parts_y, width_y, width_z)
    along_y = jnp.einsum(
        "csxjlam,sjaty->cxtlmy", blocks, y_table, preferred_element_type=jnp.float32
    ).astype(jnp.bfloat16)
    return jnp.einsum(
        "cxtlmy,tlmz->cxyz", along_y, z_table, preferred_element_type=jnp.float32
    ).astype(jnp.bfloat16)


def to_spectral(field, ky_count, mode_count):
    channels, span_x, span_y, length = field.shape
    parts_x = lax.axis_size("px")
    parts_y = lax.axis_size("py")
    width_y = ky_count // parts_x
    width_z = mode_count // parts_y
    order_y = box_order(length, span_y)
    order_z = box_order(length, length)
    forward = complex_table(length, -1.0)
    y_table = (
        mode_table(mode_ids(ky_count, length), length, -1.0)
        .transpose(0, 3, 2, 1)[:, order_y]
        .reshape(2, length, 2, parts_x, width_y)
    )
    z_table = real_table(length, mode_count)[..., order_z].reshape(2, parts_y, width_z, length)
    along_z = jnp.einsum(
        "cxyz,rlmz->crlmxy", field, z_table, preferred_element_type=jnp.float32
    ).astype(jnp.bfloat16)
    along_y = jnp.einsum(
        "crlmxy,rysja->csxjlam", along_z, y_table, preferred_element_type=jnp.float32
    ).astype(jnp.bfloat16)
    along_y = along_y.reshape(channels, 2, span_x, parts_x * parts_y, width_y * width_z)
    moved = lax.all_to_all(along_y, ("px", "py"), split_axis=3, concat_axis=2, tiled=True)
    number = moved.shape[0]
    flat = moved.reshape(number, 2, length, -1)
    along_x = jnp.einsum("csxp,sxtn->ctpn", flat, forward, preferred_element_type=jnp.float32)
    return along_x.reshape(number, 2, width_y, width_z, length)


def to_boxes(field):
    channels, span_x, span_y, span_z = field.shape
    tiles = field.reshape(
        channels, span_x // PATCH, PATCH, PATCH, span_y // PATCH, PATCH, span_z // PATCH
    )
    return tiles.transpose(0, 2, 3, 5, 1, 4, 6).reshape(channels * PATCH**3, -1)


def from_boxes(box_values, layout):
    channels, span_x, span_y, span_z = layout
    tiles = box_values.reshape(
        channels, PATCH, PATCH, PATCH, span_x // PATCH, span_y // PATCH, span_z // PATCH
    )
    return tiles.transpose(0, 4, 1, 2, 5, 3, 6).reshape(layout)


def closure_terms(velocity, force_adj, w_in, b_in, w_out):
    features = to_boxes(velocity)
    adjoints = to_boxes(force_adj)
    pre_act = jnp.dot(w_in, features, preferred_element_type=jnp.float32) + b_in[:, None]
    hidden = jax.nn.silu(pre_act).astype(jnp.bfloat16)
    sigmoid = jax.nn.sigmoid(pre_act)
    hidden_adj = FORCING * jnp.dot(w_out.T, adjoints, preferred_element_type=jnp.float32)
    pre_adj = (hidden_adj * sigmoid * (1.0 + pre_act * (1.0 - sigmoid))).astype(jnp.bfloat16)
    grad_in = jnp.dot(pre_adj, features.T, preferred_element_type=jnp.float32)
    grad_out = FORCING * jnp.dot(adjoints, hidden.T, preferred_element_type=jnp.float32)
    grad_bias = jnp.sum(pre_adj.astype(jnp.float32), axis=1)[None, :]
    feat_adj = jnp.dot(w_in.T, pre_adj, preferred_element_type=jnp.float32).astype(jnp.bfloat16)
    feat_adj = lax.optimization_barrier(from_boxes(feat_adj, velocity.shape))
    return (feat_adj, grad_in, grad_out, grad_bias)


def field_cross(former, latter):
    return cross(
        [former[slot].astype(jnp.float32) for slot in range(3)],
        [latter[slot].astype(jnp.float32) for slot in range(3)],
    )


def shards(state, cotangent, w_in, b_in, w_out):
    width_y = state.shape[2]
    width_z = state.shape[3]
    length = state.shape[4]
    ky_count = width_y * lax.axis_size("px")
    ky_ids = lax.axis_index("px") * width_y + jnp.arange(width_y, dtype=jnp.int32)
    kz_ids = lax.axis_index("py") * width_z + jnp.arange(width_z, dtype=jnp.int32)
    waves, retained, damping, weight, square = factors(ky_ids, kz_ids, length, ky_count)
    kept = retained * state
    force_spec = TIME_STEP * retained * project(waves, square, damping * cotangent)
    modes = width_z * lax.axis_size("py")
    force_adj = to_physical(force_spec)
    velocity = to_physical(weight * kept)
    vorticity = to_physical(weight * curl_modes(waves, kept))
    vort_adj = jnp.stack(field_cross(force_adj, velocity)).astype(jnp.bfloat16)
    spec_vort = to_spectral(vort_adj, ky_count, modes)
    feat_adj, grad_in, grad_out, grad_bias = closure_terms(velocity, force_adj, w_in, b_in, w_out)
    turned = field_cross(vorticity, force_adj)
    vel_adj = jnp.stack([feat_adj[slot].astype(jnp.float32) + turned[slot] for slot in range(3)])
    spec_vel = to_spectral(vel_adj.astype(jnp.bfloat16), ky_count, modes)
    state_grad = damping * cotangent + weight * retained * (
        spec_vel + curl_modes(waves, spec_vort)
    )
    grad_in, grad_out, grad_bias = (
        lax.psum_scatter(grad_in, ("px", "py"), scatter_dimension=0, tiled=True),
        lax.psum_scatter(grad_out, ("px", "py"), scatter_dimension=1, tiled=True),
        lax.psum_scatter(grad_bias, ("px", "py"), scatter_dimension=1, tiled=True),
    )
    return (state_grad, grad_in, grad_out, grad_bias)


def solution(mesh):
    return jax.shard_map(
        shards,
        mesh=mesh,
        in_specs=(
            P("rep", None, "px", "py", None),
            P("rep", None, "px", "py", None),
            P(),
            P(),
            P(),
        ),
        out_specs=(
            P("rep", None, "px", "py", None),
            P(("px", "py"), "rep"),
            P("rep", ("px", "py")),
            P("rep", ("px", "py")),
        ),
        check_vma=False,
    )
```
